32 devices in a mesh: groups: 2 (over x), feat: 16 (over z, y, core).
Axes of the slice: x: 2, y: 2, z: 4, core: 2. Of those that a mesh axis runs over, the one named last changes fastest.
Arguments:
- inputs: bfloat16 [512, 2048], P('groups', 'feat'), parts along dimension 0, may hold values from -70 to 70
- norm_gains: float32 [2, 2048], P(None, 'feat'), may hold values from 0.1 to 1.9
- left_factors: bfloat16 [2, 16, 128, 128], P(None, 'feat'), may hold values from -0.5 to 0.5
- right_factors: bfloat16 [2, 128, 16, 16], P(None, 'feat'), may hold values from -1 to 1
- cotangent: bfloat16 [512, 2048], P('groups', 'feat'), parts along dimension 0, may hold values from -6 to 6
Outputs:
- output: bfloat16 [512, 2048], P('groups', 'feat'), parts along dimension 0
- grad_inputs: bfloat16 [512, 2048], P('groups', 'feat'), parts along dimension 0
- grad_gains: float32 [4, 2048], P('groups', 'feat'), parts along dimension 0
- grad_left: float32 [4, 16, 128, 128], P('groups', 'feat'), parts along dimension 0
- grad_right: float32 [4, 128, 16, 16], P('groups', 'feat'), parts along dimension 0
The draws below stay inside these ranges and needn't reach their ends.
There are 2 independent parts, one for each index of `groups`. The reference program is written for one: setup_inputs(seed, part) draws one part's arguments, and reference() takes and returns one part's arrays. A program takes and returns all parts, laid end to end along the dimension named above; an argument that names none is the same for every part. Nothing has to cross between parts.
All inputs are finite; a program needn't handle non-finite values.
Results may differ from the reference program's by a relative error of at most 0.015.
Values may be sent and summed in bfloat16 or wider, within the bound.
A program may use at most 64 MiB of HBM per device.

```python
import jax
import jax.numpy as jnp
from jax import lax

NB = 16
BS = 128
D = 2048
ROWS = 256


def draw_inputs(key, part):
    key_base = jax.random.fold_in(key, 11)
    key_core, key_cols, key_rows = jax.random.split(key_base, 3)
    position = jnp.arange(D, dtype=jnp.float32) / D
    col_scale = 10.0 ** (0.8 * position - 0.4 + 0.25 * jax.random.uniform(key_cols, (D,), jnp.float32, -1.0, 1.0))
    row_scale = 10.0 ** jax.random.uniform(key_rows, (ROWS, 1), jnp.float32, -0.5, 0.5)
    core_draw = jax.random.truncated_normal(key_core, -4.0, 4.0, (ROWS, D), jnp.float32)
    return (core_draw * row_scale * col_scale[None, :]).astype(jnp.bfloat16)


def draw_right_factors(key, part):
    key_base = jax.random.fold_in(key, 23)
    position = (jnp.arange(BS, dtype=jnp.float32) / BS).reshape(1, BS, 1, 1)
    scale = NB ** (-0.5) * 10.0 ** (0.5 * position - 0.25)
    core_draw = jax.random.truncated_normal(key_base, -4.0, 4.0, (2, BS, NB, NB), jnp.float32)
    return jnp.clip(core_draw * scale, -1.0, 1.0).astype(jnp.bfloat16)


def block_levels(own_key, shape, cuts, low, top_value):
    def one(dim, shards_of):
        heights = jax.random.uniform(jax.random.fold_in(jax.random.fold_in(own_key, 6), dim), (shards_of,), jnp.float32, low / len(cuts), top_value / len(cuts))
        return jnp.repeat(jnp.exp(heights), shape[dim] // shards_of).reshape((-1,) + (1,) * (len(shape) - dim - 1))

    loudness = one(*cuts[0])
    for cut in cuts[1:]:
        loudness = loudness * one(*cut)
    return loudness


def scatter_about(rng, shape, spread, limit, pieces=(), kind=jnp.bfloat16):
    drawn = spread * jax.random.normal(rng, shape, jnp.float32)
    if pieces:
        drawn = drawn * block_levels(rng, shape, pieces, -0.22, 0.18)
    return jnp.clip(drawn, -limit, limit).astype(kind)


def setup_inputs(seed: int = 0, part: int = 0) -> dict:
    key_of = jax.random.split(jax.random.key(seed), 6)
    part_splits = jax.random.split(jax.random.fold_in(key_of[5], part), 6)
    return {
        "inputs": draw_inputs(jax.random.fold_in(jax.random.fold_in(key_of[5], part), 71), part),
        "norm_gains": jnp.clip(1.0 + 0.18 * jax.random.normal(key_of[1], (2, D), jnp.float32), 0.1, 1.9),
        "left_factors": scatter_about(key_of[2], (2, NB, BS, BS), BS ** -0.5, 0.5, ((1, 16),)),
        "right_factors": draw_right_factors(jax.random.fold_in(key_of[5], 71), part),
        "cotangent": scatter_about(part_splits[4], (ROWS, D), 1.0, 6.0, ((1, 16),)),
    }


epsilon = 1e-05
inv_root_two = 0.7071067811865476
inv_root_two_pi = 0.3989422804014327

def gelu_parts(pre):
    normal_cdf = 0.5 * (1.0 + jax.scipy.special.erf(pre * inv_root_two))
    normal_pdf = jnp.exp(-0.5 * pre * pre) * inv_root_two_pi
    return (pre * normal_cdf, normal_cdf + pre * normal_pdf)

def forward_layer(activation, gain, left, right):
    row_count = activation.shape[0]
    values = activation.astype(jnp.float32)
    inv_rms = lax.rsqrt(lax.optimization_barrier(jnp.sum(values * values, axis=1, keepdims=True)) / D + epsilon)
    normed = (values * inv_rms * gain[None, :]).astype(jnp.bfloat16).reshape(row_count, NB, BS)
    first_mix = jnp.einsum('rbi,bij->rbj', normed.astype(jnp.float32), left.astype(jnp.float32)).astype(jnp.bfloat16)
    pre = jnp.einsum('rbj,jbk->rjk', first_mix.astype(jnp.float32), right.astype(jnp.float32))
    gelu_value, gelu_slope = gelu_parts(pre)
    result = gelu_value.reshape(row_count, D).astype(jnp.bfloat16)
    return (result, (values, inv_rms, normed, first_mix, gelu_slope))

def backward_layer(upstream, stored, gain, left, right):
    values, inv_rms, normed, first_mix, gelu_slope = stored
    row_count = upstream.shape[0]
    grad_pre = (upstream.astype(jnp.float32).reshape(row_count, BS, NB) * gelu_slope).astype(jnp.bfloat16)
    grad_right = jnp.einsum('rbj,rjk->jbk', first_mix.astype(jnp.float32), grad_pre.astype(jnp.float32))
    grad_mix = jnp.einsum('rjk,jbk->rbj', grad_pre.astype(jnp.float32), right.astype(jnp.float32)).astype(jnp.bfloat16)
    grad_normed = jnp.einsum('rbj,bij->rbi', grad_mix.astype(jnp.float32), left.astype(jnp.float32)).reshape(row_count, D)
    grad_left = jnp.einsum('rbi,rbj->bij', normed.astype(jnp.float32), grad_mix.astype(jnp.float32))
    scaled = grad_normed * gain[None, :]
    inner_sum = lax.optimization_barrier(jnp.sum(values * scaled, axis=1, keepdims=True))
    grad_in = (inv_rms * scaled - values * (inv_rms * inv_rms * inv_rms) * inner_sum / D).astype(jnp.bfloat16)
    grad_gain = lax.optimization_barrier(jnp.sum(grad_normed * values * inv_rms, axis=0))
    return (grad_in, grad_gain, grad_left, grad_right)

def reference(inputs, norm_gains, left_factors, right_factors, cotangent):
    block_rows = min(ROWS, 1024)
    block_count = ROWS // block_rows

    def block_step(accum, blocks):
        in_block, cot_block = blocks
        first_out, first_kept = forward_layer(in_block, norm_gains[0], left_factors[0], right_factors[0])
        second_out, second_kept = forward_layer(first_out, norm_gains[1], left_factors[1], right_factors[1])
        upper_grad, gain_two, left_two, right_two = backward_layer(cot_block, second_kept, norm_gains[1], left_factors[1], right_factors[1])
        grad_in, gain_one, left_one, right_one = backward_layer(upper_grad, first_kept, norm_gains[0], left_factors[0], right_factors[0])
        accum = (accum[0] + jnp.stack([gain_one, gain_two]), accum[1] + jnp.stack([left_one, left_two]), accum[2] + jnp.stack([right_one, right_two]))
        return (accum, (second_out, grad_in))
    start = (jnp.zeros((2, D), jnp.float32), jnp.zeros((2, NB, BS, BS), jnp.float32), jnp.zeros((2, BS, NB, NB), jnp.float32))
    accum, (outputs, grads) = lax.scan(block_step, start, (inputs.reshape(block_count, block_rows, D), cotangent.reshape(block_count, block_rows, D)))
    return (outputs.reshape(ROWS, D), grads.reshape(ROWS, D), accum[0], accum[1], accum[2])
```

```python
import functools

import jax
import jax.numpy as jnp
from jax import lax
from jax.experimental import pallas as pl
from jax.experimental.pallas import tpu as pltpu
from jax.sharding import PartitionSpec as P

BS = 128


epsilon = 1e-05
inv_root_two = 0.7071067811865476
inv_root_two_pi = 0.3989422804014327


def gelu_parts(pre):
    normal_cdf = 0.5 * (1.0 + jax.scipy.special.erf(pre * inv_root_two))
    normal_pdf = jnp.exp(-0.5 * pre * pre) * inv_root_two_pi
    return (pre * normal_cdf, normal_cdf + pre * normal_pdf)


def forward_layer(activation, gain, left, right):
    row_count = activation.shape[0]
    owned_blocks = left.shape[0]
    full_width = activation.shape[1] * lax.axis_size("feat")
    values = activation.astype(jnp.float32)
    totals = lax.psum(jnp.sum(values * values, axis=1, keepdims=True), "feat")
    inv_rms = lax.rsqrt(totals / full_width + epsilon)
    normed = (
        (values * inv_rms * gain[None, :]).astype(jnp.bfloat16).reshape(row_count, owned_blocks, BS)
    )
    first_mix = jnp.einsum("rbi,bij->rbj", normed, left, preferred_element_type=jnp.float32).astype(
        jnp.bfloat16
    )
    received = lax.all_to_all(first_mix, "feat", split_axis=2, concat_axis=1, tiled=True)
    pre_part = jnp.einsum("rbj,jbk->rjk", received, right, preferred_element_type=jnp.float32)
    gelu_value, gelu_slope = gelu_parts(pre_part)
    result = gelu_value.reshape(row_count, -1).astype(jnp.bfloat16)
    return (result, (values, inv_rms, normed, received, gelu_slope))


def backward_layer(upstream, stored, gain, left, right):
    values, inv_rms, normed, exchanged, gelu_slope = stored
    row_count = upstream.shape[0]
    owned_blocks = right.shape[0]
    block_count = right.shape[2]
    full_width = values.shape[1] * lax.axis_size("feat")
    grad_pre = (
        upstream.astype(jnp.float32).reshape(row_count, owned_blocks, block_count) * gelu_slope
    ).astype(jnp.bfloat16)
    grad_right = jnp.einsum("rbj,rjk->jbk", exchanged, grad_pre, preferred_element_type=jnp.float32)
    grad_mix = jnp.einsum(
        "rjk,jbk->rbj", grad_pre, right, preferred_element_type=jnp.float32
    ).astype(jnp.bfloat16)
    returned = lax.all_to_all(grad_mix, "feat", split_axis=1, concat_axis=2, tiled=True)
    grad_normed = jnp.einsum("rbj,bij->rbi", returned, left, preferred_element_type=jnp.float32)
    grad_left = jnp.einsum("rbi,rbj->bij", normed, returned, preferred_element_type=jnp.float32)
    grad_normed = grad_normed.reshape(row_count, -1)
    scaled = grad_normed * gain[None, :]
    inner_sum = lax.psum(jnp.sum(values * scaled, axis=1, keepdims=True), "feat")
    grad_in = (
        inv_rms * scaled - values * (inv_rms * inv_rms * inv_rms) * inner_sum / full_width
    ).astype(jnp.bfloat16)
    grad_gain = jnp.sum(grad_normed * values * inv_rms, axis=0)
    return (grad_in, grad_gain, grad_left, grad_right)


def body(inputs, norm_gains, left_factors, right_factors, cotangent):
    activation = inputs
    saved_all = []
    for layer_pos in range(2):
        activation, stored = forward_layer(
            activation, norm_gains[layer_pos], left_factors[layer_pos], right_factors[layer_pos]
        )
        saved_all.append(stored)
    upstream = cotangent
    gain_grads = [None, None]
    left_grads = [None, None]
    right_grads = [None, None]
    for layer_pos in (1, 0):
        upstream, grad_gain, grad_left, grad_right = backward_layer(
            upstream,
            saved_all[layer_pos],
            norm_gains[layer_pos],
            left_factors[layer_pos],
            right_factors[layer_pos],
        )
        gain_grads[layer_pos] = grad_gain
        left_grads[layer_pos] = grad_left
        right_grads[layer_pos] = grad_right
    return (
        activation,
        upstream,
        jnp.stack(gain_grads),
        jnp.stack(left_grads),
        jnp.stack(right_grads),
    )


def dot_plain(lhs, rhs):
    return lax.dot_general(lhs, rhs, (((1,), (0,)), ((), ())), preferred_element_type=jnp.float32)


def dot_left_transposed(lhs, rhs):
    return lax.dot_general(lhs, rhs, (((0,), (0,)), ((), ())), preferred_element_type=jnp.float32)


def dot_right_transposed(lhs, rhs):
    return lax.dot_general(lhs, rhs, (((1,), (1,)), ((), ())), preferred_element_type=jnp.float32)


def one_hot(condition):
    return jnp.where(condition, 1.0, 0.0).astype(jnp.bfloat16)


def iotas(rows, cols):
    return (
        lax.broadcasted_iota(jnp.int32, (rows, cols), 0),
        lax.broadcasted_iota(jnp.int32, (rows, cols), 1),
    )


def fused_kernel(
    peers,
    x_ref,
    gains_ref,
    left_ref,
    right_ref,
    cot_ref,
    out_ref,
    gin_ref,
    ggain_ref,
    gleft_ref,
    gright_ref,
    send_ref,
    recv_ref,
    stat_ref,
    stats_ref,
    send_sem,
    recv_sem,
    stat_send_sem,
    stat_recv_sem,
):
    rows, width = x_ref.shape
    half = rows // 2
    own_j, blocks, kk = right_ref.shape[1:]
    full_width = width * peers
    me = lax.axis_index("feat")

    barrier = pltpu.get_barrier_semaphore()
    for step in range(1, peers):
        pl.semaphore_signal(
            barrier,
            inc=1,
            device_id={"feat": lax.rem(me + step, peers)},
            device_id_type=pl.DeviceIdType.MESH,
        )

    def copies(turn, step):
        peer = lax.rem(me + step, peers)
        data = pltpu.make_async_remote_copy(
            src_ref=send_ref.at[turn, peer],
            dst_ref=recv_ref.at[turn, me],
            send_sem=send_sem.at[turn, step],
            recv_sem=recv_sem.at[turn, step],
            device_id={"feat": peer},
            device_id_type=pl.DeviceIdType.MESH,
        )
        stat = pltpu.make_async_remote_copy(
            src_ref=stat_ref.at[turn],
            dst_ref=stats_ref.at[turn, me],
            send_sem=stat_send_sem.at[turn, step],
            recv_sem=stat_recv_sem.at[turn, step],
            device_id={"feat": peer},
            device_id_type=pl.DeviceIdType.MESH,
        )
        return data, stat

    def start(turn, value, stat):
        slabs = value.reshape(peers, own_j, rows)
        slabs = jnp.concatenate([slabs[:, :, :half], slabs[:, :, half:]], axis=1)
        send_ref[turn] = slabs.astype(jnp.bfloat16)
        stat_ref[turn] = stat
        for step in range(1, peers):
            for copy in copies(turn, step):
                copy.start()
        recv_ref[turn, pl.ds(me, 1)] = send_ref[turn, pl.ds(me, 1)]
        stats_ref[turn, pl.ds(me, 1)] = stat_ref[turn].reshape(1, 1, rows)

    def finish(turn):
        for step in range(1, peers):
            for copy in copies(turn, step):
                copy.wait()
        got = recv_ref[turn].astype(jnp.float32)
        got = jnp.concatenate([got[:, :own_j], got[:, own_j:]], axis=2)
        got = got.reshape(peers * own_j, rows)
        return got, jnp.sum(stats_ref[turn], axis=0)

    row_id, col_id = iotas(width, width)
    gain_cols = [
        jnp.sum(
            jnp.where(row_id == col_id, gains_ref[layer : layer + 1, :], 0.0),
            axis=1,
            keepdims=True,
        )
        for layer in range(2)
    ]
    lefts = [left_ref[layer, 0] for layer in range(2)]
    gained = [
        (lefts[layer].astype(jnp.float32) * gain_cols[layer]).astype(jnp.bfloat16)
        for layer in range(2)
    ]
    act0 = x_ref[...].astype(jnp.float32).T
    mixed0 = dot_left_transposed(gained[0], act0.astype(jnp.bfloat16))
    square0 = jnp.sum(act0 * act0, axis=0, keepdims=True)

    pl.semaphore_wait(barrier, peers - 1)
    start(0, mixed0, square0)

    pick_r, pick_c = iotas(width, kk)
    pick_k = one_hot(pick_r % kk == pick_c)
    same_j = row_id // kk == col_id // blocks
    spread = one_hot(row_id % blocks == col_id // own_j)
    on_j = row_id // kk == col_id % own_j
    right_mats = []
    for layer in range(2):
        flat = right_ref[layer].reshape(own_j * blocks, kk)
        by_k = jnp.where(same_j, dot_right_transposed(pick_k, flat), 0.0).astype(jnp.bfloat16)
        mat = jnp.where(on_j, dot_plain(by_k, spread), 0.0).astype(jnp.bfloat16)
        right_mats.append(mat)
    reorder = one_hot((col_id // own_j == row_id % blocks) & (col_id % own_j == row_id // blocks))
    keep_j = row_id // blocks == col_id // kk
    cot = cot_ref[...].astype(jnp.float32).T

    def forward(turn, layer):
        got, total = finish(turn)
        inv_rms = lax.rsqrt(total / full_width + epsilon)
        raw = dot_plain(right_mats[layer], got.astype(jnp.bfloat16))
        pre = raw * inv_rms
        cdf = 0.5 * (1.0 + lax.erf(pre * inv_root_two))
        return got, inv_rms, raw, pre, cdf

    def slope_of(pre, cdf):
        return cdf + pre * (jnp.exp(-0.5 * pre * pre) * inv_root_two_pi)

    def right_grad(layer, got, inv_rms, grad_pre):
        exchanged = (got * inv_rms).astype(jnp.bfloat16)
        ordered = dot_plain(reorder, exchanged).astype(jnp.bfloat16)
        prods = dot_right_transposed(ordered, grad_pre)
        prods = jnp.where(keep_j, prods, 0.0)
        shift = width // 2
        while shift >= kk:
            prods = prods + pltpu.roll(prods, shift, 1)
            shift //= 2
        gright_ref[layer] = prods[:, :kk].reshape(own_j, blocks, kk)

    def backward(turn, layer, act, inv_rms):
        got, inner = finish(turn)
        got = got.astype(jnp.bfloat16)
        grad_normed = dot_plain(lefts[layer], got)
        scaled = grad_normed * gain_cols[layer]
        upstream = inv_rms * scaled - act * (inv_rms * inv_rms * inv_rms) * inner / full_width
        return got, grad_normed, upstream

    def left_grads(layer, act, inv_rms, got, grad_normed):
        centred = act * inv_rms
        normed = (centred * gain_cols[layer]).astype(jnp.bfloat16)
        gleft_ref[layer, 0] = dot_right_transposed(normed, got)
        column = jnp.sum(grad_normed * centred, axis=1, keepdims=True)
        ggain_ref[layer : layer + 1, :] = jnp.sum(
            jnp.where(row_id == col_id, column, 0.0), axis=0, keepdims=True
        )

    got1, inv1, raw1, pre1, cdf1 = forward(0, 0)
    act1_low = (pre1 * cdf1).astype(jnp.bfloat16)
    act1 = act1_low.astype(jnp.float32)
    start(1, dot_left_transposed(gained[1], act1_low), jnp.sum(act1 * act1, axis=0, keepdims=True))
    slope1 = slope_of(pre1, cdf1)
    inv0 = inv1

    got2, inv2, raw2, pre2, cdf2 = forward(1, 1)
    grad_pre2 = (cot * slope_of(pre2, cdf2)).astype(jnp.bfloat16)
    start(
        2,
        dot_left_transposed(right_mats[1], grad_pre2),
        jnp.sum(grad_pre2.astype(jnp.float32) * raw2, axis=0, keepdims=True),
    )
    out_ref[...] = (pre2 * cdf2).T.astype(out_ref.dtype)
    right_grad(1, got2, inv2, grad_pre2)

    back2, grad_normed2, up1 = backward(2, 1, act1, inv2)
    up1 = up1.astype(jnp.bfloat16).astype(jnp.float32)
    grad_pre1 = (up1 * slope1).astype(jnp.bfloat16)
    start(
        3,
        dot_left_transposed(right_mats[0], grad_pre1),
        jnp.sum(grad_pre1.astype(jnp.float32) * raw1, axis=0, keepdims=True),
    )
    right_grad(0, got1, inv0, grad_pre1)
    left_grads(1, act1, inv2, back2, grad_normed2)

    back1, grad_normed1, up0 = backward(3, 0, act0, inv0)
    gin_ref[...] = up0.T.astype(gin_ref.dtype)
    left_grads(0, act0, inv0, back1, grad_normed1)


def device_body(peers, inputs, norm_gains, left_factors, right_factors, cotangent):
    rows, width = inputs.shape
    own_j, blocks, kk = right_factors.shape[1:]
    args = (inputs, norm_gains, left_factors, right_factors, cotangent)
    fits = (
        rows == 2 * BS
        and width == BS
        and left_factors.shape[1] == 1
        and blocks == peers
        and own_j % 8 == 0
        and kk % 8 == 0
    )
    if not fits:
        return body(*args)
    half = rows // 2
    turns = 4
    vmem = pl.BlockSpec(memory_space=pltpu.VMEM)
    return pl.pallas_call(
        functools.partial(fused_kernel, peers),
        out_shape=(
            jax.ShapeDtypeStruct((rows, width), jnp.bfloat16),
            jax.ShapeDtypeStruct((rows, width), jnp.bfloat16),
            jax.ShapeDtypeStruct(norm_gains.shape, jnp.float32),
            jax.ShapeDtypeStruct(left_factors.shape, jnp.float32),
            jax.ShapeDtypeStruct(right_factors.shape, jnp.float32),
        ),
        in_specs=[vmem] * 5,
        out_specs=(vmem,) * 5,
        scratch_shapes=[
            pltpu.VMEM((turns, peers, 2 * own_j, half), jnp.bfloat16),
            pltpu.VMEM((turns, peers, 2 * own_j, half), jnp.bfloat16),
            pltpu.VMEM((turns, 1, rows), jnp.float32),
            pltpu.VMEM((turns, peers, 1, rows), jnp.float32),
            pltpu.SemaphoreType.DMA((turns, peers)),
            pltpu.SemaphoreType.DMA((turns, peers)),
            pltpu.SemaphoreType.DMA((turns, peers)),
            pltpu.SemaphoreType.DMA((turns, peers)),
        ],
        compiler_params=pltpu.CompilerParams(collective_id=0, has_side_effects=True),
    )(*args)


def solution(mesh):
    return jax.shard_map(
        functools.partial(device_body, mesh.shape["feat"]),
        mesh=mesh,
        in_specs=(
            P("groups", "feat"),
            P(None, "feat"),
            P(None, "feat", None, None),
            P(None, "feat", None, None),
            P("groups", "feat"),
        ),
        out_specs=(
            P("groups", "feat"),
            P("groups", "feat"),
            P("groups", "feat"),
            P("groups", "feat", None, None),
            P("groups", "feat", None, None),
        ),
        check_vma=False,
    )
```

```python
import functools

import jax
import jax.numpy as jnp
from jax import lax
from jax.experimental import pallas as pl
from jax.experimental.pallas import tpu as pltpu
from jax.sharding import PartitionSpec as P

BS = 128


epsilon = 1e-05
inv_root_two = 0.7071067811865476
inv_root_two_pi = 0.3989422804014327


def gelu_parts(pre):
    normal_cdf = 0.5 * (1.0 + jax.scipy.special.erf(pre * inv_root_two))
    normal_pdf = jnp.exp(-0.5 * pre * pre) * inv_root_two_pi
    return (pre * normal_cdf, normal_cdf + pre * normal_pdf)


def forward_layer(activation, gain, left, right):
    row_count = activation.shape[0]
    owned_blocks = left.shape[0]
    full_width = activation.shape[1] * lax.axis_size("feat")
    values = activation.astype(jnp.float32)
    totals = lax.psum(jnp.sum(values * values, axis=1, keepdims=True), "feat")
    inv_rms = lax.rsqrt(totals / full_width + epsilon)
    normed = (
        (values * inv_rms * gain[None, :]).astype(jnp.bfloat16).reshape(row_count, owned_blocks, BS)
    )
    first_mix = jnp.einsum("rbi,bij->rbj", normed, left, preferred_element_type=jnp.float32).astype(
        jnp.bfloat16
    )
    received = lax.all_to_all(first_mix, "feat", split_axis=2, concat_axis=1, tiled=True)
    pre_part = jnp.einsum("rbj,jbk->rjk", received, right, preferred_element_type=jnp.float32)
    gelu_value, gelu_slope = gelu_parts(pre_part)
    result = gelu_value.reshape(row_count, -1).astype(jnp.bfloat16)
    return (result, (values, inv_rms, normed, received, gelu_slope))


def backward_layer(upstream, stored, gain, left, right):
    values, inv_rms, normed, exchanged, gelu_slope = stored
    row_count = upstream.shape[0]
    owned_blocks = right.shape[0]
    block_count = right.shape[2]
    full_width = values.shape[1] * lax.axis_size("feat")
    grad_pre = (
        upstream.astype(jnp.float32).reshape(row_count, owned_blocks, block_count) * gelu_slope
    ).astype(jnp.bfloat16)
    grad_right = jnp.einsum("rbj,rjk->jbk", exchanged, grad_pre, preferred_element_type=jnp.float32)
    grad_mix = jnp.einsum(
        "rjk,jbk->rbj", grad_pre, right, preferred_element_type=jnp.float32
    ).astype(jnp.bfloat16)
    returned = lax.all_to_all(grad_mix, "feat", split_axis=1, concat_axis=2, tiled=True)
    grad_normed = jnp.einsum("rbj,bij->rbi", returned, left, preferred_element_type=jnp.float32)
    grad_left = jnp.einsum("rbi,rbj->bij", normed, returned, preferred_element_type=jnp.float32)
    grad_normed = grad_normed.reshape(row_count, -1)
    scaled = grad_normed * gain[None, :]
    inner_sum = lax.psum(jnp.sum(values * scaled, axis=1, keepdims=True), "feat")
    grad_in = (
        inv_rms * scaled - values * (inv_rms * inv_rms * inv_rms) * inner_sum / full_width
    ).astype(jnp.bfloat16)
    grad_gain = jnp.sum(grad_normed * values * inv_rms, axis=0)
    return (grad_in, grad_gain, grad_left, grad_right)


def body(inputs, norm_gains, left_factors, right_factors, cotangent):
    activation = inputs
    saved_all = []
    for layer_pos in range(2):
        activation, stored = forward_layer(
            activation, norm_gains[layer_pos], left_factors[layer_pos], right_factors[layer_pos]
        )
        saved_all.append(stored)
    upstream = cotangent
    gain_grads = [None, None]
    left_grads = [None, None]
    right_grads = [None, None]
    for layer_pos in (1, 0):
        upstream, grad_gain, grad_left, grad_right = backward_layer(
            upstream,
            saved_all[layer_pos],
            norm_gains[layer_pos],
            left_factors[layer_pos],
            right_factors[layer_pos],
        )
        gain_grads[layer_pos] = grad_gain
        left_grads[layer_pos] = grad_left
        right_grads[layer_pos] = grad_right
    return (
        activation,
        upstream,
        jnp.stack(gain_grads),
        jnp.stack(left_grads),
        jnp.stack(right_grads),
    )


def dot_plain(lhs, rhs):
    return lax.dot_general(lhs, rhs, (((1,), (0,)), ((), ())), preferred_element_type=jnp.float32)


def dot_left_transposed(lhs, rhs):
    return lax.dot_general(lhs, rhs, (((0,), (0,)), ((), ())), preferred_element_type=jnp.float32)


def dot_right_transposed(lhs, rhs):
    return lax.dot_general(lhs, rhs, (((1,), (1,)), ((), ())), preferred_element_type=jnp.float32)


def one_hot(condition):
    return jnp.where(condition, 1.0, 0.0).astype(jnp.bfloat16)


def iotas(rows, cols):
    return (
        lax.broadcasted_iota(jnp.int32, (rows, cols), 0),
        lax.broadcasted_iota(jnp.int32, (rows, cols), 1),
    )


def fused_kernel(
    peers,
    x_any,
    gains_any,
    left_any,
    right_any,
    cot_any,
    out_ref,
    gin_ref,
    ggain_ref,
    gleft_ref,
    gright_ref,
    x_ref,
    gains_ref,
    left_ref,
    right_ref,
    cot_ref,
    load_sem,
    send_ref,
    recv_ref,
    stat_ref,
    stats_ref,
    send_sem,
    recv_sem,
    stat_send_sem,
    stat_recv_sem,
):
    loads = [
        pltpu.make_async_copy(source, target, load_sem.at[place])
        for place, (source, target) in enumerate(
            (
                (x_any, x_ref),
                (gains_any, gains_ref),
                (left_any, left_ref),
                (right_any, right_ref),
                (cot_any, cot_ref),
            )
        )
    ]
    for load in loads:
        load.start()
    rows, width = x_ref.shape
    half = rows // 2
    own_j, blocks, kk = right_ref.shape[1:]
    full_width = width * peers
    me = lax.axis_index("feat")

    barrier = pltpu.get_barrier_semaphore()
    for step in range(1, peers):
        pl.semaphore_signal(
            barrier,
            inc=1,
            device_id={"feat": lax.rem(me + step, peers)},
            device_id_type=pl.DeviceIdType.MESH,
        )

    for load in loads:
        load.wait()

    def copies(turn, step):
        peer = lax.rem(me + step, peers)
        data = pltpu.make_async_remote_copy(
            src_ref=send_ref.at[turn, peer],
            dst_ref=recv_ref.at[turn, me],
            send_sem=send_sem.at[turn, step],
            recv_sem=recv_sem.at[turn, step],
            device_id={"feat": peer},
            device_id_type=pl.DeviceIdType.MESH,
        )
        stat = pltpu.make_async_remote_copy(
            src_ref=stat_ref.at[turn],
            dst_ref=stats_ref.at[turn, me],
            send_sem=stat_send_sem.at[turn, step],
            recv_sem=stat_recv_sem.at[turn, step],
            device_id={"feat": peer},
            device_id_type=pl.DeviceIdType.MESH,
        )
        return data, stat

    def start(turn, value, stat):
        slabs = value.reshape(peers, own_j, rows)
        slabs = jnp.concatenate([slabs[:, :, :half], slabs[:, :, half:]], axis=1)
        send_ref[turn] = slabs.astype(jnp.bfloat16)
        stat_ref[turn] = stat
        for step in sorted(range(1, peers), key=lambda gap: abs(gap - peers // 2)):
            for copy in copies(turn, step):
                copy.start()
        recv_ref[turn, pl.ds(me, 1)] = send_ref[turn, pl.ds(me, 1)]
        stats_ref[turn, pl.ds(me, 1)] = stat_ref[turn].reshape(1, 1, rows)

    def finish(turn):
        for step in range(1, peers):
            for copy in copies(turn, step):
                copy.wait()
        got = recv_ref[turn].astype(jnp.float32)
        got = jnp.concatenate([got[:, :own_j], got[:, own_j:]], axis=2)
        got = got.reshape(peers * own_j, rows)
        return got, jnp.sum(stats_ref[turn], axis=0)

    row_id, col_id = iotas(width, width)
    gain_cols = [
        jnp.sum(
            jnp.where(row_id == col_id, gains_ref[layer : layer + 1, :], 0.0),
            axis=1,
            keepdims=True,
        )
        for layer in range(2)
    ]
    lefts = [left_ref[layer, 0] for layer in range(2)]
    gained = [
        (lefts[layer].astype(jnp.float32) * gain_cols[layer]).astype(jnp.bfloat16)
        for layer in range(2)
    ]
    act0 = x_ref[...].astype(jnp.float32).T
    mixed0 = dot_left_transposed(gained[0], act0.astype(jnp.bfloat16))
    square0 = jnp.sum(act0 * act0, axis=0, keepdims=True)

    pl.semaphore_wait(barrier, peers - 1)
    start(0, mixed0, square0)

    pick_r, pick_c = iotas(width, kk)
    pick_k = one_hot(pick_r % kk == pick_c)
    same_j = row_id // kk == col_id // blocks
    spread = one_hot(row_id % blocks == col_id // own_j)
    on_j = row_id // kk == col_id % own_j
    right_mats = []
    for layer in range(2):
        flat = right_ref[layer].reshape(own_j * blocks, kk)
        by_k = jnp.where(same_j, dot_right_transposed(pick_k, flat), 0.0).astype(jnp.bfloat16)
        mat = jnp.where(on_j, dot_plain(by_k, spread), 0.0).astype(jnp.bfloat16)
        right_mats.append(mat)
    reorder = one_hot((col_id // own_j == row_id % blocks) & (col_id % own_j == row_id // blocks))
    keep_j = row_id // blocks == col_id // kk
    cot = cot_ref[...].astype(jnp.float32).T

    def forward(turn, layer):
        got, total = finish(turn)
        inv_rms = lax.rsqrt(total / full_width + epsilon)
        raw = dot_plain(right_mats[layer], got.astype(jnp.bfloat16))
        pre = raw * inv_rms
        cdf = 0.5 * (1.0 + lax.erf(pre * inv_root_two))
        return got, inv_rms, raw, pre, cdf

    def slope_of(pre, cdf):
        return cdf + pre * (jnp.exp(-0.5 * pre * pre) * inv_root_two_pi)

    def right_grad(layer, got, inv_rms, grad_pre):
        exchanged = (got * inv_rms).astype(jnp.bfloat16)
        ordered = dot_plain(reorder, exchanged).astype(jnp.bfloat16)
        prods = dot_right_transposed(ordered, grad_pre)
        prods = jnp.where(keep_j, prods, 0.0)
        shift = width // 2
        while shift >= kk:
            prods = prods + pltpu.roll(prods, shift, 1)
            shift //= 2
        gright_ref[layer] = prods[:, :kk].reshape(own_j, blocks, kk)

    def backward(turn, layer, act, inv_rms):
        got, inner = finish(turn)
        got = got.astype(jnp.bfloat16)
        grad_normed = dot_plain(lefts[layer], got)
        scaled = grad_normed * gain_cols[layer]
        upstream = inv_rms * scaled - act * (inv_rms * inv_rms * inv_rms) * inner / full_width
        return got, grad_normed, upstream

    def left_grads(layer, act, inv_rms, got, grad_normed):
        centred = act * inv_rms
        normed = (centred * gain_cols[layer]).astype(jnp.bfloat16)
        gleft_ref[layer, 0] = dot_right_transposed(normed, got)
        column = jnp.sum(grad_normed * centred, axis=1, keepdims=True)
        ggain_ref[layer : layer + 1, :] = jnp.sum(
            jnp.where(row_id == col_id, column, 0.0), axis=0, keepdims=True
        )

    got1, inv1, raw1, pre1, cdf1 = forward(0, 0)
    act1_low = (pre1 * cdf1).astype(jnp.bfloat16)
    act1 = act1_low.astype(jnp.float32)
    start(1, dot_left_transposed(gained[1], act1_low), jnp.sum(act1 * act1, axis=0, keepdims=True))
    slope1 = slope_of(pre1, cdf1)
    inv0 = inv1

    got2, inv2, raw2, pre2, cdf2 = forward(1, 1)
    grad_pre2 = (cot * slope_of(pre2, cdf2)).astype(jnp.bfloat16)
    start(
        2,
        dot_left_transposed(right_mats[1], grad_pre2),
        jnp.sum(grad_pre2.astype(jnp.float32) * raw2, axis=0, keepdims=True),
    )
    out_ref[...] = (pre2 * cdf2).T.astype(out_ref.dtype)
    right_grad(1, got2, inv2, grad_pre2)

    back2, grad_normed2, up1 = backward(2, 1, act1, inv2)
    up1 = up1.astype(jnp.bfloat16).astype(jnp.float32)
    grad_pre1 = (up1 * slope1).astype(jnp.bfloat16)
    start(
        3,
        dot_left_transposed(right_mats[0], grad_pre1),
        jnp.sum(grad_pre1.astype(jnp.float32) * raw1, axis=0, keepdims=True),
    )
    right_grad(0, got1, inv0, grad_pre1)
    left_grads(1, act1, inv2, back2, grad_normed2)

    back1, grad_normed1, up0 = backward(3, 0, act0, inv0)
    gin_ref[...] = up0.T.astype(gin_ref.dtype)
    left_grads(0, act0, inv0, back1, grad_normed1)


def write_kernel(*refs):
    sources, targets, sem = refs[:5], refs[5:10], refs[10]
    writes = [
        pltpu.make_async_copy(source, target, sem.at[place])
        for place, (source, target) in enumerate(zip(sources, targets))
    ]
    for write in writes:
        write.start()
    for write in writes:
        write.wait()


def device_body(peers, inputs, norm_gains, left_factors, right_factors, cotangent):
    rows, width = inputs.shape
    own_j, blocks, kk = right_factors.shape[1:]
    args = (inputs, norm_gains, left_factors, right_factors, cotangent)
    fits = (
        rows == 2 * BS
        and width == BS
        and left_factors.shape[1] == 1
        and blocks == peers
        and own_j % 8 == 0
        and kk % 8 == 0
    )
    if not fits:
        return body(*args)
    half = rows // 2
    turns = 4
    vmem = pl.BlockSpec(memory_space=pltpu.VMEM)
    in_hbm = pl.BlockSpec(memory_space=pltpu.HBM)
    shapes = (
        ((rows, width), jnp.bfloat16),
        ((rows, width), jnp.bfloat16),
        (norm_gains.shape, jnp.float32),
        (left_factors.shape, jnp.float32),
        (right_factors.shape, jnp.float32),
    )
    results = pl.pallas_call(
        functools.partial(fused_kernel, peers),
        out_shape=tuple(pltpu.VMEM(*shape) for shape in shapes),
        in_specs=[in_hbm] * 5,
        out_specs=(vmem,) * 5,
        scratch_shapes=[pltpu.VMEM(arg.shape, arg.dtype) for arg in args]
        + [
            pltpu.SemaphoreType.DMA((len(args),)),
            pltpu.VMEM((turns, peers, 2 * own_j, half), jnp.bfloat16),
            pltpu.VMEM((turns, peers, 2 * own_j, half), jnp.bfloat16),
            pltpu.VMEM((turns, 1, rows), jnp.float32),
            pltpu.VMEM((turns, peers, 1, rows), jnp.float32),
            pltpu.SemaphoreType.DMA((turns, peers)),
            pltpu.SemaphoreType.DMA((turns, peers)),
            pltpu.SemaphoreType.DMA((turns, peers)),
            pltpu.SemaphoreType.DMA((turns, peers)),
        ],
        compiler_params=pltpu.CompilerParams(
            collective_id=0, has_side_effects=True, vmem_limit_bytes=16 * 2**20
        ),
    )(*(pltpu.with_memory_space_constraint(arg, pltpu.HBM) for arg in args))
    return pl.pallas_call(
        write_kernel,
        out_shape=tuple(pltpu.HBM(*shape) for shape in shapes),
        in_specs=[vmem] * 5,
        out_specs=(in_hbm,) * 5,
        scratch_shapes=[pltpu.SemaphoreType.DMA((5,))],
        compiler_params=pltpu.CompilerParams(vmem_limit_bytes=4 * 2**20),
    )(*(pltpu.with_memory_space_constraint(result, pltpu.VMEM) for result in results))


def solution(mesh):
    return jax.shard_map(
        functools.partial(device_body, mesh.shape["feat"]),
        mesh=mesh,
        in_specs=(
            P("groups", "feat"),
            P(None, "feat"),
            P(None, "feat", None, None),
            P(None, "feat", None, None),
            P("groups", "feat"),
        ),
        out_specs=(
            P("groups", "feat"),
            P("groups", "feat"),
            P("groups", "feat"),
            P("groups", "feat", None, None),
            P("groups", "feat", None, None),
        ),
        check_vma=False,
    )
```

```python
import functools

import jax
import jax.numpy as jnp
from jax import lax
from jax.experimental import pallas as pl
from jax.experimental.pallas import tpu as pltpu
from jax.sharding import PartitionSpec as P

BS = 128


epsilon = 1e-05
inv_root_two = 0.7071067811865476
inv_root_two_pi = 0.3989422804014327


def gelu_parts(pre):
    normal_cdf = 0.5 * (1.0 + jax.scipy.special.erf(pre * inv_root_two))
    normal_pdf = jnp.exp(-0.5 * pre * pre) * inv_root_two_pi
    return (pre * normal_cdf, normal_cdf + pre * normal_pdf)


def forward_layer(activation, gain, left, right):
    row_count = activation.shape[0]
    owned_blocks = left.shape[0]
    full_width = activation.shape[1] * lax.axis_size("feat")
    values = activation.astype(jnp.float32)
    totals = lax.psum(jnp.sum(values * values, axis=1, keepdims=True), "feat")
    inv_rms = lax.rsqrt(totals / full_width + epsilon)
    normed = (
        (values * inv_rms * gain[None, :]).astype(jnp.bfloat16).reshape(row_count, owned_blocks, BS)
    )
    first_mix = jnp.einsum("rbi,bij->rbj", normed, left, preferred_element_type=jnp.float32).astype(
        jnp.bfloat16
    )
    received = lax.all_to_all(first_mix, "feat", split_axis=2, concat_axis=1, tiled=True)
    pre_part = jnp.einsum("rbj,jbk->rjk", received, right, preferred_element_type=jnp.float32)
    gelu_value, gelu_slope = gelu_parts(pre_part)
    result = gelu_value.reshape(row_count, -1).astype(jnp.bfloat16)
    return (result, (values, inv_rms, normed, received, gelu_slope))


def backward_layer(upstream, stored, gain, left, right):
    values, inv_rms, normed, exchanged, gelu_slope = stored
    row_count = upstream.shape[0]
    owned_blocks = right.shape[0]
    block_count = right.shape[2]
    full_width = values.shape[1] * lax.axis_size("feat")
    grad_pre = (
        upstream.astype(jnp.float32).reshape(row_count, owned_blocks, block_count) * gelu_slope
    ).astype(jnp.bfloat16)
    grad_right = jnp.einsum("rbj,rjk->jbk", exchanged, grad_pre, preferred_element_type=jnp.float32)
    grad_mix = jnp.einsum(
        "rjk,jbk->rbj", grad_pre, right, preferred_element_type=jnp.float32
    ).astype(jnp.bfloat16)
    returned = lax.all_to_all(grad_mix, "feat", split_axis=1, concat_axis=2, tiled=True)
    grad_normed = jnp.einsum("rbj,bij->rbi", returned, left, preferred_element_type=jnp.float32)
    grad_left = jnp.einsum("rbi,rbj->bij", normed, returned, preferred_element_type=jnp.float32)
    grad_normed = grad_normed.reshape(row_count, -1)
    scaled = grad_normed * gain[None, :]
    inner_sum = lax.psum(jnp.sum(values * scaled, axis=1, keepdims=True), "feat")
    grad_in = (
        inv_rms * scaled - values * (inv_rms * inv_rms * inv_rms) * inner_sum / full_width
    ).astype(jnp.bfloat16)
    grad_gain = jnp.sum(grad_normed * values * inv_rms, axis=0)
    return (grad_in, grad_gain, grad_left, grad_right)


def body(inputs, norm_gains, left_factors, right_factors, cotangent):
    activation = inputs
    saved_all = []
    for layer_pos in range(2):
        activation, stored = forward_layer(
            activation, norm_gains[layer_pos], left_factors[layer_pos], right_factors[layer_pos]
        )
        saved_all.append(stored)
    upstream = cotangent
    gain_grads = [None, None]
    left_grads = [None, None]
    right_grads = [None, None]
    for layer_pos in (1, 0):
        upstream, grad_gain, grad_left, grad_right = backward_layer(
            upstream,
            saved_all[layer_pos],
            norm_gains[layer_pos],
            left_factors[layer_pos],
            right_factors[layer_pos],
        )
        gain_grads[layer_pos] = grad_gain
        left_grads[layer_pos] = grad_left
        right_grads[layer_pos] = grad_right
    return (
        activation,
        upstream,
        jnp.stack(gain_grads),
        jnp.stack(left_grads),
        jnp.stack(right_grads),
    )


def dot_plain(lhs, rhs):
    return lax.dot_general(lhs, rhs, (((1,), (0,)), ((), ())), preferred_element_type=jnp.float32)


def dot_left_transposed(lhs, rhs):
    return lax.dot_general(lhs, rhs, (((0,), (0,)), ((), ())), preferred_element_type=jnp.float32)


def dot_right_transposed(lhs, rhs):
    return lax.dot_general(lhs, rhs, (((1,), (1,)), ((), ())), preferred_element_type=jnp.float32)


def one_hot(condition):
    return jnp.where(condition, 1.0, 0.0).astype(jnp.bfloat16)


def iotas(rows, cols):
    return (
        lax.broadcasted_iota(jnp.int32, (rows, cols), 0),
        lax.broadcasted_iota(jnp.int32, (rows, cols), 1),
    )


def fused_kernel(
    peers,
    x_any,
    gains_any,
    left_any,
    right_any,
    cot_any,
    out_ref,
    gin_ref,
    ggain_ref,
    gleft_ref,
    gright_ref,
    x_ref,
    gains_ref,
    left_ref,
    right_ref,
    cot_ref,
    load_sem,
    send_ref,
    recv_ref,
    stat_ref,
    stats_ref,
    send_sem,
    recv_sem,
    stat_send_sem,
    stat_recv_sem,
):
    loads = [
        pltpu.make_async_copy(source, target, load_sem.at[place])
        for place, (source, target) in enumerate(
            (
                (x_any, x_ref),
                (gains_any, gains_ref),
                (left_any, left_ref),
                (right_any, right_ref),
                (cot_any, cot_ref),
            )
        )
    ]
    for load in loads:
        load.start()
    rows, width = x_ref.shape
    half = rows // 2
    own_j, blocks, kk = right_ref.shape[1:]
    full_width = width * peers
    me = lax.axis_index("feat")

    barrier = pltpu.get_barrier_semaphore()
    for step in range(1, peers):
        pl.semaphore_signal(
            barrier,
            inc=1,
            device_id={"feat": lax.rem(me + step, peers)},
            device_id_type=pl.DeviceIdType.MESH,
        )

    for load in loads[:3]:
        load.wait()

    flips = [bit * (1 - 2 * (me // bit % 2)) for bit in (1 << p for p in range(peers.bit_length() - 1))]

    def partner(step):
        return me + sum(flip for place, flip in enumerate(flips) if step >> place & 1)

    def copies(turn, step):
        peer = partner(step)
        data = pltpu.make_async_remote_copy(
            src_ref=send_ref.at[turn, peer],
            dst_ref=recv_ref.at[turn, me],
            send_sem=send_sem.at[turn, step],
            recv_sem=recv_sem.at[turn, step],
            device_id={"feat": peer},
            device_id_type=pl.DeviceIdType.MESH,
        )
        stat = pltpu.make_async_remote_copy(
            src_ref=stat_ref.at[turn],
            dst_ref=stats_ref.at[turn, me],
            send_sem=stat_send_sem.at[turn, step],
            recv_sem=stat_recv_sem.at[turn, step],
            device_id={"feat": peer},
            device_id_type=pl.DeviceIdType.MESH,
        )
        return data, stat

    def stage(turn, value, stat):
        slabs = value.reshape(peers, own_j, rows)
        slabs = jnp.concatenate([slabs[:, :, :half], slabs[:, :, half:]], axis=1)
        send_ref[turn] = slabs.astype(jnp.bfloat16)
        stat_ref[turn] = stat

    def launch(turn):
        for step in range(peers - 1, 0, -1):
            for copy in copies(turn, step):
                copy.start()
        recv_ref[turn, pl.ds(me, 1)] = send_ref[turn, pl.ds(me, 1)]
        stats_ref[turn, pl.ds(me, 1)] = stat_ref[turn].reshape(1, 1, rows)

    def start(turn, value, stat):
        stage(turn, value, stat)
        launch(turn)

    def finish(turn):
        for step in range(1, peers):
            for copy in copies(turn, step):
                copy.wait()
        got = recv_ref[turn].astype(jnp.float32)
        got = jnp.concatenate([got[:, :own_j], got[:, own_j:]], axis=2)
        got = got.reshape(peers * own_j, rows)
        return got, jnp.sum(stats_ref[turn], axis=0)

    row_id, col_id = iotas(width, width)
    gain_cols = [
        jnp.sum(
            jnp.where(row_id == col_id, gains_ref[layer : layer + 1, :], 0.0),
            axis=1,
            keepdims=True,
        )
        for layer in range(2)
    ]
    lefts = [left_ref[layer, 0] for layer in range(2)]
    gained = [
        (lefts[layer].astype(jnp.float32) * gain_cols[layer]).astype(jnp.bfloat16)
        for layer in range(2)
    ]
    act0 = x_ref[...].astype(jnp.float32).T
    mixed0 = dot_left_transposed(gained[0], act0.astype(jnp.bfloat16))
    square0 = jnp.sum(act0 * act0, axis=0, keepdims=True)

    stage(0, mixed0, square0)
    pl.semaphore_wait(barrier, peers - 1)
    launch(0)

    for load in loads[3:]:
        load.wait()

    pick_r, pick_c = iotas(width, kk)
    pick_k = one_hot(pick_r % kk == pick_c)
    same_j = row_id // kk == col_id // blocks
    spread = one_hot(row_id % blocks == col_id // own_j)
    on_j = row_id // kk == col_id % own_j
    right_mats = []
    for layer in range(2):
        flat = right_ref[layer].reshape(own_j * blocks, kk)
        by_k = jnp.where(same_j, dot_right_transposed(pick_k, flat), 0.0).astype(jnp.bfloat16)
        mat = jnp.where(on_j, dot_plain(by_k, spread), 0.0).astype(jnp.bfloat16)
        right_mats.append(mat)
    reorder = one_hot((col_id // own_j == row_id % blocks) & (col_id % own_j == row_id // blocks))
    keep_j = row_id // blocks == col_id // kk
    cot = cot_ref[...].astype(jnp.float32).T

    def forward(turn, layer):
        got, total = finish(turn)
        inv_rms = lax.rsqrt(total / full_width + epsilon)
        raw = dot_plain(right_mats[layer], got.astype(jnp.bfloat16))
        pre = raw * inv_rms
        cdf = 0.5 * (1.0 + lax.erf(pre * inv_root_two))
        return got, inv_rms, raw, pre, cdf

    def slope_of(pre, cdf):
        return cdf + pre * (jnp.exp(-0.5 * pre * pre) * inv_root_two_pi)

    def right_grad(layer, got, inv_rms, grad_pre):
        exchanged = (got * inv_rms).astype(jnp.bfloat16)
        ordered = dot_plain(reorder, exchanged).astype(jnp.bfloat16)
        prods = dot_right_transposed(ordered, grad_pre)
        prods = jnp.where(keep_j, prods, 0.0)
        shift = width // 2
        while shift >= kk:
            prods = prods + pltpu.roll(prods, shift, 1)
            shift //= 2
        gright_ref[layer] = prods[:, :kk].reshape(own_j, blocks, kk)

    def backward_factors(layer, act, inv_rms):
        centred = act * inv_rms
        return (
            inv_rms * gain_cols[layer],
            centred * (inv_rms * inv_rms / full_width),
            centred,
            (centred * gain_cols[layer]).astype(jnp.bfloat16),
        )

    def backward(turn, layer, factors):
        got, inner = finish(turn)
        got = got.astype(jnp.bfloat16)
        grad_normed = dot_plain(lefts[layer], got)
        return got, grad_normed, factors[0] * grad_normed - factors[1] * inner

    def left_grads(layer, factors, got, grad_normed):
        gleft_ref[layer, 0] = dot_right_transposed(factors[3], got)
        column = jnp.sum(grad_normed * factors[2], axis=1, keepdims=True)
        ggain_ref[layer : layer + 1, :] = jnp.sum(
            jnp.where(row_id == col_id, column, 0.0), axis=0, keepdims=True
        )

    got1, inv1, raw1, pre1, cdf1 = forward(0, 0)
    act1_low = (pre1 * cdf1).astype(jnp.bfloat16)
    act1 = act1_low.astype(jnp.float32)
    start(1, dot_left_transposed(gained[1], act1_low), jnp.sum(act1 * act1, axis=0, keepdims=True))
    slope1 = slope_of(pre1, cdf1)
    inv0 = inv1

    got2, inv2, raw2, pre2, cdf2 = forward(1, 1)
    grad_pre2 = (cot * slope_of(pre2, cdf2)).astype(jnp.bfloat16)
    start(
        2,
        dot_left_transposed(right_mats[1], grad_pre2),
        jnp.sum(grad_pre2.astype(jnp.float32) * raw2, axis=0, keepdims=True),
    )
    out_ref[...] = (pre2 * cdf2).T.astype(out_ref.dtype)
    right_grad(1, got2, inv2, grad_pre2)

    factors2 = backward_factors(1, act1, inv2)
    back2, grad_normed2, up1 = backward(2, 1, factors2)
    up1 = up1.astype(jnp.bfloat16).astype(jnp.float32)
    grad_pre1 = (up1 * slope1).astype(jnp.bfloat16)
    start(
        3,
        dot_left_transposed(right_mats[0], grad_pre1),
        jnp.sum(grad_pre1.astype(jnp.float32) * raw1, axis=0, keepdims=True),
    )
    right_grad(0, got1, inv0, grad_pre1)
    left_grads(1, factors2, back2, grad_normed2)

    factors1 = backward_factors(0, act0, inv0)
    back1, grad_normed1, up0 = backward(3, 0, factors1)
    gin_ref[...] = up0.astype(gin_ref.dtype).T
    left_grads(0, factors1, back1, grad_normed1)


def write_kernel(*refs):
    sources, targets, sem = refs[:5], refs[5:10], refs[10]
    writes = [
        pltpu.make_async_copy(source, target, sem.at[place])
        for place, (source, target) in enumerate(zip(sources, targets))
    ]
    for write in writes:
        write.start()
    for write in writes:
        write.wait()


def device_body(peers, inputs, norm_gains, left_factors, right_factors, cotangent):
    rows, width = inputs.shape
    own_j, blocks, kk = right_factors.shape[1:]
    args = (inputs, norm_gains, left_factors, right_factors, cotangent)
    fits = (
        rows == 2 * BS
        and width == BS
        and left_factors.shape[1] == 1
        and blocks == peers
        and peers & (peers - 1) == 0
        and own_j % 8 == 0
        and kk % 8 == 0
    )
    if not fits:
        return body(*args)
    half = rows // 2
    turns = 4
    vmem = pl.BlockSpec(memory_space=pltpu.VMEM)
    in_hbm = pl.BlockSpec(memory_space=pltpu.HBM)
    shapes = (
        ((rows, width), jnp.bfloat16),
        ((rows, width), jnp.bfloat16),
        (norm_gains.shape, jnp.float32),
        (left_factors.shape, jnp.float32),
        (right_factors.shape, jnp.float32),
    )
    results = pl.pallas_call(
        functools.partial(fused_kernel, peers),
        out_shape=tuple(pltpu.VMEM(*shape) for shape in shapes),
        in_specs=[in_hbm] * 5,
        out_specs=(vmem,) * 5,
        scratch_shapes=[pltpu.VMEM(arg.shape, arg.dtype) for arg in args]
        + [
            pltpu.SemaphoreType.DMA((len(args),)),
            pltpu.VMEM((turns, peers, 2 * own_j, half), jnp.bfloat16),
            pltpu.VMEM((turns, peers, 2 * own_j, half), jnp.bfloat16),
            pltpu.VMEM((turns, 1, rows), jnp.float32),
            pltpu.VMEM((turns, peers, 1, rows), jnp.float32),
            pltpu.SemaphoreType.DMA((turns, peers)),
            pltpu.SemaphoreType.DMA((turns, peers)),
            pltpu.SemaphoreType.DMA((turns, peers)),
            pltpu.SemaphoreType.DMA((turns, peers)),
        ],
        compiler_params=pltpu.CompilerParams(
            collective_id=0, has_side_effects=True, vmem_limit_bytes=16 * 2**20
        ),
    )(*(pltpu.with_memory_space_constraint(arg, pltpu.HBM) for arg in args))
    return pl.pallas_call(
        write_kernel,
        out_shape=tuple(pltpu.HBM(*shape) for shape in shapes),
        in_specs=[vmem] * 5,
        out_specs=(in_hbm,) * 5,
        scratch_shapes=[pltpu.SemaphoreType.DMA((5,))],
        compiler_params=pltpu.CompilerParams(vmem_limit_bytes=4 * 2**20),
    )(*(pltpu.with_memory_space_constraint(result, pltpu.VMEM) for result in results))


def solution(mesh):
    return jax.shard_map(
        functools.partial(device_body, mesh.shape["feat"]),
        mesh=mesh,
        in_specs=(
            P("groups", "feat"),
            P(None, "feat"),
            P(None, "feat", None, None),
            P(None, "feat", None, None),
            P("groups", "feat"),
        ),
        out_specs=(
            P("groups", "feat"),
            P("groups", "feat"),
            P("groups", "feat"),
            P("groups", "feat", None, None),
            P("groups", "feat", None, None),
        ),
        check_vma=False,
    )
```

```python
import functools

import jax
import jax.numpy as jnp
from jax import lax
from jax.experimental import pallas as pl
from jax.experimental.pallas import tpu as pltpu
from jax.sharding import PartitionSpec as P

BS = 128


epsilon = 1e-05
inv_root_two = 0.7071067811865476
inv_root_two_pi = 0.3989422804014327


def gelu_parts(pre):
    normal_cdf = 0.5 * (1.0 + jax.scipy.special.erf(pre * inv_root_two))
    normal_pdf = jnp.exp(-0.5 * pre * pre) * inv_root_two_pi
    return (pre * normal_cdf, normal_cdf + pre * normal_pdf)


def forward_layer(activation, gain, left, right):
    row_count = activation.shape[0]
    owned_blocks = left.shape[0]
    full_width = activation.shape[1] * lax.axis_size("feat")
    values = activation.astype(jnp.float32)
    totals = lax.psum(jnp.sum(values * values, axis=1, keepdims=True), "feat")
    inv_rms = lax.rsqrt(totals / full_width + epsilon)
    normed = (
        (values * inv_rms * gain[None, :]).astype(jnp.bfloat16).reshape(row_count, owned_blocks, BS)
    )
    first_mix = jnp.einsum("rbi,bij->rbj", normed, left, preferred_element_type=jnp.float32).astype(
        jnp.bfloat16
    )
    received = lax.all_to_all(first_mix, "feat", split_axis=2, concat_axis=1, tiled=True)
    pre_part = jnp.einsum("rbj,jbk->rjk", received, right, preferred_element_type=jnp.float32)
    gelu_value, gelu_slope = gelu_parts(pre_part)
    result = gelu_value.reshape(row_count, -1).astype(jnp.bfloat16)
    return (result, (values, inv_rms, normed, received, gelu_slope))


def backward_layer(upstream, stored, gain, left, right):
    values, inv_rms, normed, exchanged, gelu_slope = stored
    row_count = upstream.shape[0]
    owned_blocks = right.shape[0]
    block_count = right.shape[2]
    full_width = values.shape[1] * lax.axis_size("feat")
    grad_pre = (
        upstream.astype(jnp.float32).reshape(row_count, owned_blocks, block_count) * gelu_slope
    ).astype(jnp.bfloat16)
    grad_right = jnp.einsum("rbj,rjk->jbk", exchanged, grad_pre, preferred_element_type=jnp.float32)
    grad_mix = jnp.einsum(
        "rjk,jbk->rbj", grad_pre, right, preferred_element_type=jnp.float32
    ).astype(jnp.bfloat16)
    returned = lax.all_to_all(grad_mix, "feat", split_axis=1, concat_axis=2, tiled=True)
    grad_normed = jnp.einsum("rbj,bij->rbi", returned, left, preferred_element_type=jnp.float32)
    grad_left = jnp.einsum("rbi,rbj->bij", normed, returned, preferred_element_type=jnp.float32)
    grad_normed = grad_normed.reshape(row_count, -1)
    scaled = grad_normed * gain[None, :]
    inner_sum = lax.psum(jnp.sum(values * scaled, axis=1, keepdims=True), "feat")
    grad_in = (
        inv_rms * scaled - values * (inv_rms * inv_rms * inv_rms) * inner_sum / full_width
    ).astype(jnp.bfloat16)
    grad_gain = jnp.sum(grad_normed * values * inv_rms, axis=0)
    return (grad_in, grad_gain, grad_left, grad_right)


def body(inputs, norm_gains, left_factors, right_factors, cotangent):
    activation = inputs
    saved_all = []
    for layer_pos in range(2):
        activation, stored = forward_layer(
            activation, norm_gains[layer_pos], left_factors[layer_pos], right_factors[layer_pos]
        )
        saved_all.append(stored)
    upstream = cotangent
    gain_grads = [None, None]
    left_grads = [None, None]
    right_grads = [None, None]
    for layer_pos in (1, 0):
        upstream, grad_gain, grad_left, grad_right = backward_layer(
            upstream,
            saved_all[layer_pos],
            norm_gains[layer_pos],
            left_factors[layer_pos],
            right_factors[layer_pos],
        )
        gain_grads[layer_pos] = grad_gain
        left_grads[layer_pos] = grad_left
        right_grads[layer_pos] = grad_right
    return (
        activation,
        upstream,
        jnp.stack(gain_grads),
        jnp.stack(left_grads),
        jnp.stack(right_grads),
    )


def dot_plain(lhs, rhs):
    return lax.dot_general(lhs, rhs, (((1,), (0,)), ((), ())), preferred_element_type=jnp.float32)


def dot_left_transposed(lhs, rhs):
    return lax.dot_general(lhs, rhs, (((0,), (0,)), ((), ())), preferred_element_type=jnp.float32)


def dot_right_transposed(lhs, rhs):
    return lax.dot_general(lhs, rhs, (((1,), (1,)), ((), ())), preferred_element_type=jnp.float32)


def one_hot(condition):
    return jnp.where(condition, 1.0, 0.0).astype(jnp.bfloat16)


def iotas(rows, cols):
    return (
        lax.broadcasted_iota(jnp.int32, (rows, cols), 0),
        lax.broadcasted_iota(jnp.int32, (rows, cols), 1),
    )


def fused_kernel(
    peers,
    x_any,
    gains_any,
    left_any,
    right_any,
    cot_any,
    out_ref,
    gin_ref,
    ggain_ref,
    gleft_ref,
    gright_ref,
    x_ref,
    gains_ref,
    left_ref,
    right_ref,
    cot_ref,
    load_sem,
    send_ref,
    recv_ref,
    stat_ref,
    stats_ref,
    send_sem,
    recv_sem,
    stat_send_sem,
    stat_recv_sem,
):
    loads = [
        pltpu.make_async_copy(source, target, load_sem.at[place])
        for place, (source, target) in enumerate(
            (
                (x_any, x_ref),
                (gains_any, gains_ref),
                (left_any, left_ref),
                (right_any, right_ref),
                (cot_any, cot_ref),
            )
        )
    ]
    rows, width = x_ref.shape
    half = rows // 2
    own_j, blocks, kk = right_ref.shape[1:]
    full_width = width * peers
    me = lax.axis_index("feat")

    flips = [bit * (1 - 2 * (me // bit % 2)) for bit in (1 << p for p in range(peers.bit_length() - 1))]

    def partner(step):
        return me + sum(flip for place, flip in enumerate(flips) if step >> place & 1)

    barrier = pltpu.get_barrier_semaphore()
    for step in range(peers - 1, 0, -1):
        pl.semaphore_signal(
            barrier,
            inc=1,
            device_id={"feat": partner(step)},
            device_id_type=pl.DeviceIdType.MESH,
        )

    for load in loads:
        load.start()
    for load in loads[:3]:
        load.wait()

    def copies(turn, step):
        peer = partner(step)
        data = pltpu.make_async_remote_copy(
            src_ref=send_ref.at[turn, peer],
            dst_ref=recv_ref.at[turn, me],
            send_sem=send_sem.at[turn, step],
            recv_sem=recv_sem.at[turn, step],
            device_id={"feat": peer},
            device_id_type=pl.DeviceIdType.MESH,
        )
        stat = pltpu.make_async_remote_copy(
            src_ref=stat_ref.at[turn],
            dst_ref=stats_ref.at[turn, me],
            send_sem=stat_send_sem.at[turn, step],
            recv_sem=stat_recv_sem.at[turn, step],
            device_id={"feat": peer},
            device_id_type=pl.DeviceIdType.MESH,
        )
        return data, stat

    def stage(turn, value, stat):
        slabs = value.reshape(peers, own_j, rows)
        slabs = jnp.concatenate([slabs[:, :, :half], slabs[:, :, half:]], axis=1)
        send_ref[turn] = slabs.astype(jnp.bfloat16)
        stat_ref[turn] = stat

    def launch(turn):
        for step in range(peers - 1, 0, -1):
            for copy in copies(turn, step)[::-1]:
                copy.start()
        recv_ref[turn, pl.ds(me, 1)] = send_ref[turn, pl.ds(me, 1)]
        stats_ref[turn, pl.ds(me, 1)] = stat_ref[turn].reshape(1, 1, rows)

    def start(turn, value, stat):
        stage(turn, value, stat)
        launch(turn)

    def finish(turn):
        for step in range(1, peers):
            for copy in copies(turn, step):
                copy.wait()
        got = recv_ref[turn].astype(jnp.float32)
        got = jnp.concatenate([got[:, :own_j], got[:, own_j:]], axis=2)
        got = got.reshape(peers * own_j, rows)
        return got, jnp.sum(stats_ref[turn], axis=0)

    row_id, col_id = iotas(width, width)
    gain_cols = [
        jnp.sum(
            jnp.where(row_id == col_id, gains_ref[layer : layer + 1, :], 0.0),
            axis=1,
            keepdims=True,
        )
        for layer in range(2)
    ]
    lefts = [left_ref[layer, 0] for layer in range(2)]
    gained = [
        (lefts[layer].astype(jnp.float32) * gain_cols[layer]).astype(jnp.bfloat16)
        for layer in range(2)
    ]
    act0 = x_ref[...].astype(jnp.float32).T
    mixed0 = dot_left_transposed(gained[0], act0.astype(jnp.bfloat16))
    square0 = jnp.sum(act0 * act0, axis=0, keepdims=True)

    stage(0, mixed0, square0)
    pl.semaphore_wait(barrier, peers - 1)
    launch(0)

    for load in loads[3:]:
        load.wait()

    pick_r, pick_c = iotas(width, kk)
    pick_k = one_hot(pick_r % kk == pick_c)
    same_j = row_id // kk == col_id // blocks
    spread = one_hot(row_id % blocks == col_id // own_j)
    on_j = row_id // kk == col_id % own_j
    right_mats = []
    for layer in range(2):
        flat = right_ref[layer].reshape(own_j * blocks, kk)
        by_k = jnp.where(same_j, dot_right_transposed(pick_k, flat), 0.0).astype(jnp.bfloat16)
        mat = jnp.where(on_j, dot_plain(by_k, spread), 0.0).astype(jnp.bfloat16)
        right_mats.append(mat)
    reorder = one_hot((col_id // own_j == row_id % blocks) & (col_id % own_j == row_id // blocks))
    keep_j = row_id // blocks == col_id // kk
    cot = cot_ref[...].astype(jnp.float32).T

    def forward(turn, layer):
        got, total = finish(turn)
        inv_rms = lax.rsqrt(total / full_width + epsilon)
        raw = dot_plain(right_mats[layer], got.astype(jnp.bfloat16))
        pre = raw * inv_rms
        cdf = 0.5 * (1.0 + lax.erf(pre * inv_root_two))
        return got, inv_rms, raw, pre, cdf

    def slope_of(pre, cdf):
        return cdf + pre * (jnp.exp(-0.5 * pre * pre) * inv_root_two_pi)

    def right_grad(layer, got, inv_rms, grad_pre):
        exchanged = (got * inv_rms).astype(jnp.bfloat16)
        ordered = dot_plain(reorder, exchanged).astype(jnp.bfloat16)
        prods = dot_right_transposed(ordered, grad_pre)
        prods = jnp.where(keep_j, prods, 0.0)
        shift = width // 2
        while shift >= kk:
            prods = prods + pltpu.roll(prods, shift, 1)
            shift //= 2
        gright_ref[layer] = prods[:, :kk].reshape(own_j, blocks, kk)

    def backward_factors(layer, act, inv_rms):
        centred = act * inv_rms
        return (
            inv_rms * gain_cols[layer],
            centred * (inv_rms * inv_rms / full_width),
            centred,
            (centred * gain_cols[layer]).astype(jnp.bfloat16),
        )

    def backward(turn, layer, factors):
        got, inner = finish(turn)
        got = got.astype(jnp.bfloat16)
        grad_normed = dot_plain(lefts[layer], got)
        return got, grad_normed, factors[0] * grad_normed - factors[1] * inner

    def left_grads(layer, factors, got, grad_normed):
        gleft_ref[layer, 0] = dot_right_transposed(factors[3], got)
        prods = grad_normed * factors[2]
        high = prods.astype(jnp.bfloat16)
        low = (prods - high.astype(jnp.float32)).astype(jnp.bfloat16)
        ones = jnp.ones((8, rows), jnp.bfloat16)
        sums = dot_right_transposed(ones, high) + dot_right_transposed(ones, low)
        ggain_ref[layer : layer + 1, :] = sums[:1]

    got1, inv1, raw1, pre1, cdf1 = forward(0, 0)
    act1_low = (pre1 * cdf1).astype(jnp.bfloat16)
    act1 = act1_low.astype(jnp.float32)
    start(1, dot_left_transposed(gained[1], act1_low), jnp.sum(act1 * act1, axis=0, keepdims=True))
    slope1 = slope_of(pre1, cdf1)
    inv0 = inv1

    got2, inv2, raw2, pre2, cdf2 = forward(1, 1)
    grad_pre2 = (cot * slope_of(pre2, cdf2)).astype(jnp.bfloat16)
    start(
        2,
        dot_left_transposed(right_mats[1], grad_pre2),
        jnp.sum(grad_pre2.astype(jnp.float32) * raw2, axis=0, keepdims=True),
    )
    out_ref[...] = (pre2 * cdf2).T.astype(out_ref.dtype)
    right_grad(1, got2, inv2, grad_pre2)

    factors2 = backward_factors(1, act1, inv2)
    back2, grad_normed2, up1 = backward(2, 1, factors2)
    up1 = up1.astype(jnp.bfloat16).astype(jnp.float32)
    grad_pre1 = (up1 * slope1).astype(jnp.bfloat16)
    start(
        3,
        dot_left_transposed(right_mats[0], grad_pre1),
        jnp.sum(grad_pre1.astype(jnp.float32) * raw1, axis=0, keepdims=True),
    )
    right_grad(0, got1, inv0, grad_pre1)
    left_grads(1, factors2, back2, grad_normed2)

    factors1 = backward_factors(0, act0, inv0)
    back1, grad_normed1, up0 = backward(3, 0, factors1)
    gin_ref[...] = up0.astype(gin_ref.dtype).T
    left_grads(0, factors1, back1, grad_normed1)


def write_kernel(*refs):
    sources, targets, sem = refs[:5], refs[5:10], refs[10]
    writes = [
        pltpu.make_async_copy(source, target, sem.at[place])
        for place, (source, target) in enumerate(zip(sources, targets))
    ]
    for write in writes:
        write.start()
    for write in writes:
        write.wait()


def device_body(peers, inputs, norm_gains, left_factors, right_factors, cotangent):
    rows, width = inputs.shape
    own_j, blocks, kk = right_factors.shape[1:]
    args = (inputs, norm_gains, left_factors, right_factors, cotangent)
    fits = (
        rows == 2 * BS
        and width == BS
        and left_factors.shape[1] == 1
        and blocks == peers
        and peers & (peers - 1) == 0
        and own_j % 8 == 0
        and kk % 8 == 0
    )
    if not fits:
        return body(*args)
    half = rows // 2
    turns = 4
    vmem = pl.BlockSpec(memory_space=pltpu.VMEM)
    in_hbm = pl.BlockSpec(memory_space=pltpu.HBM)
    shapes = (
        ((rows, width), jnp.bfloat16),
        ((rows, width), jnp.bfloat16),
        (norm_gains.shape, jnp.float32),
        (left_factors.shape, jnp.float32),
        (right_factors.shape, jnp.float32),
    )
    results = pl.pallas_call(
        functools.partial(fused_kernel, peers),
        out_shape=tuple(pltpu.VMEM(*shape) for shape in shapes),
        in_specs=[in_hbm] * 5,
        out_specs=(vmem,) * 5,
        scratch_shapes=[pltpu.VMEM(arg.shape, arg.dtype) for arg in args]
        + [
            pltpu.SemaphoreType.DMA((len(args),)),
            pltpu.VMEM((turns, peers, 2 * own_j, half), jnp.bfloat16),
            pltpu.VMEM((turns, peers, 2 * own_j, half), jnp.bfloat16),
            pltpu.VMEM((turns, 1, rows), jnp.float32),
            pltpu.VMEM((turns, peers, 1, rows), jnp.float32),
            pltpu.SemaphoreType.DMA((turns, peers)),
            pltpu.SemaphoreType.DMA((turns, peers)),
            pltpu.SemaphoreType.DMA((turns, peers)),
            pltpu.SemaphoreType.DMA((turns, peers)),
        ],
        compiler_params=pltpu.CompilerParams(
            collective_id=0, has_side_effects=True, vmem_limit_bytes=16 * 2**20
        ),
    )(*(pltpu.with_memory_space_constraint(arg, pltpu.HBM) for arg in args))
    return pl.pallas_call(
        write_kernel,
        out_shape=tuple(pltpu.HBM(*shape) for shape in shapes),
        in_specs=[vmem] * 5,
        out_specs=(in_hbm,) * 5,
        scratch_shapes=[pltpu.SemaphoreType.DMA((5,))],
        compiler_params=pltpu.CompilerParams(vmem_limit_bytes=4 * 2**20),
    )(*(pltpu.with_memory_space_constraint(result, pltpu.VMEM) for result in results))


def solution(mesh):
    return jax.shard_map(
        functools.partial(device_body, mesh.shape["feat"]),
        mesh=mesh,
        in_specs=(
            P("groups", "feat"),
            P(None, "feat"),
            P(None, "feat", None, None),
            P(None, "feat", None, None),
            P("groups", "feat"),
        ),
        out_specs=(
            P("groups", "feat"),
            P("groups", "feat"),
            P("groups", "feat"),
            P("groups", "feat", None, None),
            P("groups", "feat", None, None),
        ),
        check_vma=False,
    )
```
